32 devices in a mesh: seg: 8 (over z, x), rep: 4 (over y, core).
Axes of the slice: x: 2, y: 2, z: 4, core: 2. Of those that a mesh axis runs over, the one named last changes fastest.
Arguments:
- decoder_rows: bfloat16 [256, 4096], P('rep', 'seg'), may hold values from -2000 to 2000
- norm_gain: float32 [4096], replicated, may hold values from 0.5 to 1.5
- query_weight: bfloat16 [4096, 4096], P('rep', 'seg'), may hold values from -1 to 1
- key_codes: bfloat16 [4, 4096, 4096], P('rep', 'seg'), may hold values from -127 to 127, as said below
- key_scale: float32 [4, 32, 64], P('rep', 'seg'), may hold values from 0.5 to 1.5
- value_codes: bfloat16 [4, 4096, 4096], P('rep', 'seg'), may hold values from -6 to 6
- value_scale: float32 [4, 32, 64], P('rep', 'seg'), may hold values from 0.5 to 2
- enc_lengths: int32 [4], P('rep'), may hold values from 1024 to 4096
- output_weight: bfloat16 [4096, 4096], P('seg', 'rep'), may hold values from -0.09375 to 0.09375
Outputs:
- update: bfloat16 [256, 4096], P('rep', 'seg')
The draws below stay inside these ranges and needn't reach their ends.
Inputs may be any that keep to these rules, and one draw needn't show every extreme that they name: `key_codes`: codes of a block times its scale give the cached keys.
All inputs are finite; a program needn't handle non-finite values.
Results may differ from the reference program's by a relative error of at most 0.011.
Values may be sent and summed in bfloat16 or wider, within the bound.
A program may use at most 64 MiB of HBM per device.

```python
import math
import jax
import jax.numpy as jnp
from jax import lax

D = 4096
HEADS = 64
HEAD_DIM = 64
QRY = 64
SCALE_GROUP = 128
INNER = 4096
DOCS = 4
ROWS = 256
ENC = 4096
NBLK = 32


def row_values(key):
    base_key = jax.random.fold_in(key, 101)
    key_row, key_col, key_base = jax.random.split(base_key, 3)
    row_factor = jnp.exp(jax.random.uniform(key_row, (ROWS, 1), jnp.float32) * math.log(10.0))
    col_rise = jnp.exp(jnp.arange(D, dtype=jnp.float32) / D * math.log(3.0))[None, :]
    col_factor = jnp.exp(jax.random.uniform(key_col, (1, D), jnp.float32) * math.log(10.0)) * col_rise
    base = jnp.clip(jax.random.normal(key_base, (ROWS, D), jnp.float32), -6.0, 6.0)
    return base * row_factor * col_factor


def gain_values(key):
    gain_key = jax.random.fold_in(key, 202)
    return 1.0 + jnp.clip(0.1 * jax.random.normal(gain_key, (D,), jnp.float32), -0.45, 0.45)


def weight_values(key):
    weight_key = jax.random.fold_in(key, 303)
    base = jnp.clip(jax.random.normal(weight_key, (D, INNER), jnp.float32), -6.0, 6.0)
    return base / math.sqrt(D)


def draw_decoder_rows(key, part):
    return row_values(key).astype(jnp.bfloat16)


def draw_norm_gain(key, part):
    return gain_values(key)


def draw_query_weight(key, part):
    return weight_values(key).astype(jnp.bfloat16)


def draw_key_codes(key, part):
    code_key = jax.random.fold_in(key, 404)
    key_base = jax.random.fold_in(code_key, 0)
    codes = jnp.clip(0.4 * jax.random.normal(key_base, (DOCS, ENC, INNER), jnp.float32), -3.2, 3.2)
    return codes.astype(jnp.bfloat16)


def place_ends(entries, key, smallest, high):
    dims = entries.shape
    spot = [jax.random.randint(jax.random.fold_in(key, axis), (), 0, dims[axis]) for axis in range(len(dims))]
    entries = entries.at[tuple(spot)].set(smallest)
    longest = dims.index(max(dims))
    spot[longest] = (spot[longest] + 1) % dims[longest]
    return entries.at[tuple(spot)].set(high)


def level_of(rng, shape, pieces, least, largest):
    def one(position, shards_of):
        heights = jax.random.uniform(jax.random.fold_in(jax.random.fold_in(rng, 6), position), (shards_of,), jnp.float32, least / len(pieces), largest / len(pieces))
        return jnp.repeat(jnp.exp(heights), shape[position] // shards_of).reshape((-1,) + (1,) * (len(shape) - position - 1))

    factor_of = one(*pieces[0])
    for cut in pieces[1:]:
        factor_of = factor_of * one(*cut)
    return factor_of


def normal_values(stream_key, shape, scale, bound, cuts=(), held_as=jnp.bfloat16):
    gain = level_of(stream_key, shape, cuts, -0.22, 0.18) if cuts else 1.0
    values = jax.random.normal(stream_key, shape, jnp.float32) * scale * gain
    return jnp.minimum(jnp.maximum(values, -bound), bound).astype(held_as)


def setup_inputs(seed: int = 0) -> dict:
    key_of = jax.random.split(jax.random.key(seed), 10)
    decoder_rows = draw_decoder_rows(jax.random.fold_in(key_of[9], 71), 0)
    norm_gain = draw_norm_gain(jax.random.fold_in(key_of[9], 71), 0)
    query_weight = draw_query_weight(jax.random.fold_in(key_of[9], 71), 0)
    key_codes = draw_key_codes(jax.random.fold_in(key_of[9], 71), 0)
    key_scale = jnp.clip(jnp.exp(math.log(1.5) - 1.0986123 * jax.random.uniform(key_of[4], (DOCS, NBLK, HEADS), jnp.float32) ** level_of(key_of[4], (DOCS, NBLK, HEADS), ((0, 4), (1, 8)), -0.2, 0.2)), 0.5, 1.5)
    value_codes = normal_values(key_of[5], (DOCS, ENC, INNER), 1.0, 6.0, ((0, 4), (1, 8)))
    value_scale = jnp.clip(jnp.exp(math.log(2.0) - 1.3862944 * jax.random.uniform(key_of[6], (DOCS, NBLK, HEADS), jnp.float32) ** level_of(key_of[6], (DOCS, NBLK, HEADS), ((0, 4), (1, 8)), -0.2, 0.2)), 0.5, 2.0)
    enc_lengths = place_ends(jax.random.randint(key_of[7], (DOCS,), ENC // 4, ENC + 1), jax.random.fold_in(key_of[7], 1), ENC // 4, ENC).astype(jnp.int32)
    output_weight = normal_values(key_of[8], (INNER, D), INNER ** -0.5, 0.09375, ((0, 8), (1, 4)))
    return dict(decoder_rows=decoder_rows, norm_gain=norm_gain, query_weight=query_weight, key_codes=key_codes, key_scale=key_scale, value_codes=value_codes, value_scale=value_scale, enc_lengths=enc_lengths, output_weight=output_weight)


def attend_document(document_query, document_keys, document_values, document_key_scale, document_value_scale, document_length):
    query_for_head = document_query.reshape(QRY, HEADS, HEAD_DIM).transpose(1, 0, 2)
    keys_for_head = document_keys.reshape(ENC, HEADS, HEAD_DIM).transpose(1, 0, 2)
    values_for_head = document_values.reshape(ENC, HEADS, HEAD_DIM).transpose(1, 0, 2)
    usable = (jnp.arange(ENC, dtype=jnp.int32) < document_length)[None, :]

    def single_head(group_members):
        query_of_head, key_of_head, value_of_head, key_scale_of_head, value_scale_of_head = group_members
        attention_scores = jnp.dot(query_of_head, key_of_head.T, preferred_element_type=jnp.float32)
        attention_scores = attention_scores * jnp.repeat(key_scale_of_head, SCALE_GROUP)[None, :]
        attention_scores = jnp.where(usable, attention_scores, jnp.float32(-1e+30))
        peaks = lax.optimization_barrier(jnp.max(attention_scores, axis=-1, keepdims=True))
        weights = jnp.where(usable, jnp.exp(attention_scores - peaks), jnp.float32(0.0))
        totals = lax.optimization_barrier(jnp.sum(weights, axis=-1, keepdims=True))
        scaled = (weights * jnp.repeat(value_scale_of_head, SCALE_GROUP)[None, :]).astype(jnp.bfloat16)
        summed = jnp.dot(scaled, value_of_head, preferred_element_type=jnp.float32)
        return (summed / totals).astype(jnp.bfloat16)
    each_head_output = lax.map(single_head, (query_for_head, keys_for_head, values_for_head, document_key_scale.T, document_value_scale.T))
    return each_head_output.transpose(1, 0, 2).reshape(QRY, INNER)

def reference(decoder_rows, norm_gain, query_weight, key_codes, key_scale, value_codes, value_scale, enc_lengths, output_weight):
    widened = decoder_rows.astype(jnp.float32)
    variance = lax.optimization_barrier(jnp.mean(widened * widened, axis=-1, keepdims=True))
    normed = (widened * lax.rsqrt(variance + 1e-06) * norm_gain[None, :]).astype(jnp.bfloat16)
    queries = jnp.dot(normed, query_weight, preferred_element_type=jnp.float32).astype(jnp.bfloat16)
    attended_docs = []
    for doc_index in range(DOCS):
        document_query = queries[doc_index * QRY:(doc_index + 1) * QRY]
        attended_docs.append(attend_document(document_query, key_codes[doc_index], value_codes[doc_index], key_scale[doc_index], value_scale[doc_index], enc_lengths[doc_index]))
    attended = jnp.concatenate(attended_docs, axis=0)
    return jnp.dot(attended, output_weight, preferred_element_type=jnp.float32).astype(jnp.bfloat16)
```

```python
import functools

import jax
import jax.numpy as jnp
from jax import lax
from jax.experimental import pallas as pl
from jax.experimental.pallas import tpu as pltpu
from jax.sharding import PartitionSpec as P

F32 = jnp.float32
BF16 = jnp.bfloat16
LANES = 128
PART = 16
INNER_RING = 2


def spread(value):
    high = value.astype(BF16).astype(F32)
    rest = value - high
    mid = rest.astype(BF16).astype(F32)
    low = (rest - mid).astype(BF16).astype(F32)
    packed = high + pltpu.roll(mid, PART, 1) + pltpu.roll(low, 2 * PART, 1)
    return packed.astype(BF16)


def gather_spread(packed):
    wide = packed.astype(F32)
    low = pltpu.roll(wide, LANES - 2 * PART, 1)
    mid = pltpu.roll(wide, LANES - PART, 1)
    return wide + (mid + low)


def kernel(
    nseg,
    nrep,
    heads,
    rows_ref,
    gain_ref,
    wq_hbm,
    k_hbm,
    ks_ref,
    v_hbm,
    vs_ref,
    len_ref,
    wo_hbm,
    out_ref,
    wq,
    wo,
    kbuf,
    vbuf,
    xg,
    y,
    pq,
    pq_in,
    qs,
    oout,
    oin,
    ag,
    pf,
    pf32,
    rbuf,
    sbuf,
    fbuf,
    fin,
    land,
    local_sem,
    send_sem,
    recv_sem,
):
    seg = lax.axis_index("seg")
    rep = lax.axis_index("rep")
    nrow, c = rows_ref.shape
    width = gain_ref.shape[1]
    m = nseg // nrep
    nb = INNER_RING
    na = nseg // nb
    a, b = seg // nb, seg % nb
    hd = wq.shape[1] * nseg // heads
    hpl = LANES // hd
    hpb = c // hd
    pairs = c // LANES
    tokens = kbuf.shape[0]
    blocks = ks_ref.shape[1]
    blen = tokens // blocks

    state = {"k": 0}
    started = []

    def send(src, dst, to_rep, to_seg, start=True):
        k = state["k"]
        state["k"] += 1
        copy = pltpu.make_async_remote_copy(
            src_ref=src,
            dst_ref=dst,
            send_sem=send_sem.at[k],
            recv_sem=recv_sem.at[k],
            device_id={"rep": to_rep, "seg": to_seg},
            device_id_type=pl.DeviceIdType.MESH,
        )
        if start:
            copy.start()
            started.append(copy)
        return copy

    loads = {}
    lk = 0

    def load(name, src, dst):
        nonlocal lk
        copy = pltpu.make_async_copy(src, dst, local_sem.at[lk])
        lk += 1
        copy.start()
        loads[name] = copy

    load("wq", wq_hbm, wq)
    load("k", k_hbm.at[0], kbuf)
    load("v", v_hbm.at[0], vbuf)
    load("wo", wo_hbm, wo)

    to_rep, to_seg = seg // m, rep * m + seg % m
    alone = to_rep == rep
    barrier = pltpu.get_barrier_semaphore()

    def greet(r, s):
        pl.semaphore_signal(
            barrier, inc=1, device_id={"rep": r, "seg": s}, device_id_type=pl.DeviceIdType.MESH
        )

    for d in range(1, nseg):
        greet(rep, lax.rem(seg + d, nseg))
    for d in range(1, nrep):
        greet(lax.rem(rep + d, nrep), seg)

    @pl.when(jnp.logical_not(alone))
    def _():
        greet(to_rep, to_seg)

    pl.semaphore_wait(barrier, jnp.where(alone, nseg + nrep - 2, nseg + nrep - 1))

    first = send(rows_ref, xg.at[to_seg], to_rep, to_seg, start=False)

    @pl.when(jnp.logical_not(alone))
    def _():
        first.start()
        first.wait()

    @pl.when(alone)
    def _():
        xg[seg] = rows_ref[...]

    def slot(ai, bi):
        return ai * nb + bi

    def near(d):
        return lax.rem(a + d, na)

    def from_(d):
        return lax.rem(a + na - d, na)

    def gather_start(buf):
        across = [
            send(buf.at[seg], buf.at[seg], rep, slot(a, lax.rem(b + e, nb))) for e in range(1, nb)
        ]
        along = [send(buf.at[seg], buf.at[seg], rep, slot(near(d), b)) for d in range(1, na)]
        return across, along

    def pass_on(buf, d):
        block = slot(from_(d), b)
        return [
            send(buf.at[block], buf.at[block], rep, slot(a, lax.rem(b + e, nb)))
            for e in range(1, nb)
        ]

    def gather(buf, use):
        across, along = gather_start(buf)
        use(seg)
        waiting = [(copy, slot(a, lax.rem(b + nb - e, nb))) for e, copy in enumerate(across, 1)]
        for d, copy in enumerate(along, 1):
            copy.wait_recv()
            passed = pass_on(buf, d)
            for other, block in waiting:
                other.wait_recv()
                use(block)
            use(slot(from_(d), b))
            waiting = [
                (other, slot(from_(d), lax.rem(b + nb - e, nb))) for e, other in enumerate(passed, 1)
            ]
        for other, block in waiting:
            other.wait_recv()
            use(block)

    gather(xg, lambda block: None)

    lane = lax.broadcasted_iota(jnp.int32, (nrow, LANES), 1)
    for doc in range(nrep):
        total = jnp.zeros((nrow, 1), F32)
        for j in range(m):
            wide = xg[doc * m + j].astype(F32)
            total = total + jnp.sum(wide * wide, axis=1, keepdims=True)
            at = pl.multiple_of((rep * m + j) * c, LANES)
            y[doc * nrow : (doc + 1) * nrow, j * c : (j + 1) * c] = (
                wide * gain_ref[0:1, pl.ds(at, c)]
            ).astype(BF16)
        pq[doc, :, c:] = spread(jnp.where(lane == 0, total, 0.0))
    loads["wq"].wait()
    part = jnp.dot(y[...], wq[...], preferred_element_type=F32)
    for doc in range(nrep):
        pq[doc, :, :c] = part[doc * nrow : (doc + 1) * nrow].astype(BF16)
    sums = []
    for d in range(1, nrep):
        other = lax.rem(rep + d, nrep)
        sums.append(send(pq.at[other], pq_in.at[d - 1], other, seg))
    acc = pq[rep, :, :c].astype(F32)
    squares = gather_spread(pq[rep, :, c:])
    for d, copy in enumerate(sums):
        copy.wait_recv()
        acc = acc + pq_in[d, :, :c].astype(F32)
        squares = squares + gather_spread(pq_in[d, :, c:])
    inverse = lax.rsqrt(squares[:, 0:1] / width + 1e-06)
    qs[seg] = (acc * inverse).astype(BF16)

    loads["k"].wait()
    loads["v"].wait()
    position = seg * tokens + lax.broadcasted_iota(jnp.int32, (1, tokens), 1)
    bias = jnp.where(position < len_ref[0], 0.0, -1e30).astype(F32)
    turns = []

    def attend(block):
        own_turn = not turns

        def one(t, stats):
            at = pl.multiple_of(t * LANES, LANES)
            wat = pl.multiple_of(block * c + t * LANES, LANES)
            q = qs[block, :, pl.ds(at, LANES)]
            stacked = jnp.concatenate(
                [
                    jnp.where((lane >= i * hd) & (lane < (i + 1) * hd), q, jnp.zeros_like(q))
                    for i in range(hpl)
                ],
                axis=0,
            )
            scores = lax.dot_general(
                stacked,
                kbuf[:, pl.ds(wat, LANES)],
                (((1,), (1,)), ((), ())),
                preferred_element_type=F32,
            )
            scaled_rows = []
            for i in range(hpl):
                head = block * hpb + t * hpl + i
                pieces = []
                for n in range(blocks):
                    cut = slice(n * blen, (n + 1) * blen)
                    pieces.append(
                        scores[i * nrow : (i + 1) * nrow, cut] * ks_ref[0, n, head]
                        + bias[:, cut]
                    )
                top = functools.reduce(jnp.maximum, pieces)
                peak = jnp.max(top, axis=1, keepdims=True)
                weights = [jnp.exp(piece - peak) for piece in pieces]
                whole = jnp.sum(functools.reduce(jnp.add, weights), axis=1, keepdims=True)
                scaled_rows.append(
                    jnp.concatenate(
                        [(w * vs_ref[0, n, head]).astype(BF16) for n, w in enumerate(weights)],
                        axis=1,
                    )
                )
                index = t * hpl + i
                stats = jnp.where(lane == index, peak, stats)
                stats = jnp.where(lane == LANES // 2 + index, whole, stats)
            summed = jnp.dot(
                jnp.concatenate(scaled_rows, axis=0),
                vbuf[:, pl.ds(wat, LANES)],
                preferred_element_type=F32,
            )
            mine = summed[:nrow]
            for i in range(1, hpl):
                mine = jnp.where(lane >= i * hd, summed[i * nrow : (i + 1) * nrow], mine)
            oout[block, :, pl.ds(at, LANES)] = mine.astype(BF16)
            return stats

        stats = lax.fori_loop(
            0, pairs, one, jnp.zeros((nrow, LANES), F32), unroll=2 if pairs % 2 == 0 else 1
        )
        oout[block, :, c:] = spread(stats)
        if own_turn:
            turns.append(None)
        else:
            turns.append(send(oout.at[block], oin.at[len(turns) - 1], rep, block))

    gather(qs, attend)

    for copy in turns[1:]:
        copy.wait_recv()
    parts = [oout.at[seg]] + [oin.at[i] for i in range(nseg - 1)]
    stats = [gather_spread(part_ref[:, c:]) for part_ref in parts]
    largest = functools.reduce(jnp.maximum, stats)
    factors = [jnp.exp(s - largest) for s in stats]
    denominator = functools.reduce(
        jnp.add, [f * pltpu.roll(s, LANES // 2, 1) for f, s in zip(factors, stats)]
    )
    factors = [f / denominator for f in factors]
    for t in range(pairs):
        cut = slice(t * LANES, (t + 1) * LANES)
        total = None
        for f, part_ref in zip(factors, parts):
            g = f[:, t * hpl : t * hpl + 1]
            for i in range(1, hpl):
                g = jnp.where(lane >= i * hd, f[:, t * hpl + i : t * hpl + i + 1], g)
            term = g * part_ref[:, cut].astype(F32)
            total = term if total is None else total + term
        ag[rep, :, cut] = total.astype(BF16)
    shared = [
        send(ag.at[rep], ag.at[rep], lax.rem(rep + d, nrep), seg) for d in range(1, nrep)
    ]
    loads["wo"].wait()
    for copy in shared:
        copy.wait_recv()

    part = jnp.dot(
        ag[...].reshape(nrep * nrow, c), wo[...], preferred_element_type=F32
    )
    for p in range(nseg):
        doc, j = p // m, p % m
        piece = part[doc * nrow : (doc + 1) * nrow, j * c : (j + 1) * c]
        pf32[p] = piece
        pf[p] = piece.astype(BF16)
    order = list(range(1, na)) + [0]
    crossed = {}
    for d in order:
        crossed[d] = [
            send(
                pf.at[slot(near(d), lax.rem(b + e, nb))],
                rbuf.at[d, e - 1],
                rep,
                slot(a, lax.rem(b + e, nb)),
            )
            for e in range(1, nb)
        ]
    along = []
    for d in order:
        total = pf32[slot(near(d), b)]
        for e, copy in enumerate(crossed[d]):
            copy.wait_recv()
            total = total + rbuf[d, e].astype(F32)
        if d:
            sbuf[d - 1] = total.astype(BF16)
            along.append(send(sbuf.at[d - 1], fbuf.at[d - 1], rep, slot(near(d), b)))
    for d, copy in enumerate(along):
        copy.wait_recv()
        total = total + fbuf[d].astype(F32)
    fin[...] = total.astype(BF16)
    last = send(fin, land, to_rep, to_seg, start=False)

    @pl.when(jnp.logical_not(alone))
    def _():
        last.start()
        last.wait()
        out_ref[...] = land[...]

    @pl.when(alone)
    def _():
        out_ref[...] = fin[...]

    for copy in started:
        copy.wait_send()


def per_device(
    decoder_rows,
    norm_gain,
    query_weight,
    key_codes,
    key_scale,
    value_codes,
    value_scale,
    enc_lengths,
    output_weight,
):
    nseg, nrep = lax.axis_size("seg"), lax.axis_size("rep")
    nrow, c = decoder_rows.shape
    heads = key_scale.shape[2]
    tokens, inner = key_codes.shape[1:]
    assert key_codes.shape[0] == 1 and nseg % nrep == 0 and nseg % INNER_RING == 0
    na, nb = nseg // INNER_RING, INNER_RING
    copies = 2 + 2 * (nseg - 1) + 2 * (nrep - 1) + (nseg - 1) + na * (nb - 1) + na - 1
    vmem, smem, hbm = (
        pl.BlockSpec(memory_space=pltpu.VMEM),
        pl.BlockSpec(memory_space=pltpu.SMEM),
        pl.BlockSpec(memory_space=pl.ANY),
    )
    return pl.pallas_call(
        functools.partial(kernel, nseg, nrep, heads),
        out_shape=jax.ShapeDtypeStruct((nrow, c), BF16),
        in_specs=[vmem, vmem, hbm, hbm, smem, hbm, smem, smem, hbm],
        out_specs=vmem,
        scratch_shapes=[
            pltpu.VMEM(query_weight.shape, BF16),
            pltpu.VMEM(output_weight.shape, BF16),
            pltpu.VMEM((tokens, inner), BF16),
            pltpu.VMEM((tokens, inner), BF16),
            pltpu.VMEM((nseg, nrow, c), BF16),
            pltpu.VMEM((nrep * nrow, query_weight.shape[0]), BF16),
            pltpu.VMEM((nrep, nrow, c + LANES), BF16),
            pltpu.VMEM((nrep - 1, nrow, c + LANES), BF16),
            pltpu.VMEM((nseg, nrow, c), BF16),
            pltpu.VMEM((nseg, nrow, c + LANES), BF16),
            pltpu.VMEM((nseg - 1, nrow, c + LANES), BF16),
            pltpu.VMEM((nrep, nrow, c), BF16),
            pltpu.VMEM((nseg, nrow, c), BF16),
            pltpu.VMEM((nseg, nrow, c), F32),
            pltpu.VMEM((na, nb - 1, nrow, c), BF16),
            pltpu.VMEM((na - 1, nrow, c), BF16),
            pltpu.VMEM((na - 1, nrow, c), BF16),
            pltpu.VMEM((nrow, c), BF16),
            pltpu.VMEM((nrow, c), BF16),
            pltpu.SemaphoreType.DMA((4,)),
            pltpu.SemaphoreType.DMA((copies,)),
            pltpu.SemaphoreType.DMA((copies,)),
        ],
        compiler_params=pltpu.CompilerParams(
            collective_id=0, has_side_effects=True, vmem_limit_bytes=60 * 1024 * 1024
        ),
    )(
        decoder_rows,
        norm_gain.reshape(1, -1),
        query_weight,
        key_codes,
        key_scale,
        value_codes,
        value_scale,
        enc_lengths,
        output_weight,
    )


def solution(mesh):
    placed = (
        P("rep", "seg"),
        P(),
        P("rep", "seg"),
        P("rep", "seg", None),
        P("rep", "seg", None),
        P("rep", "seg", None),
        P("rep", "seg", None),
        P("rep"),
        P("seg", "rep"),
    )
    return jax.shard_map(
        per_device, mesh=mesh, in_specs=placed, out_specs=P("rep", "seg"), check_vma=False
    )
```

```python
import functools

import jax
import jax.numpy as jnp
from jax import lax
from jax.experimental import pallas as pl
from jax.experimental.pallas import tpu as pltpu
from jax.sharding import PartitionSpec as P

F32 = jnp.float32
BF16 = jnp.bfloat16
LANES = 128
PART = 16
INNER_RING = 2


def spread(value):
    high = value.astype(BF16).astype(F32)
    rest = value - high
    mid = rest.astype(BF16).astype(F32)
    low = (rest - mid).astype(BF16).astype(F32)
    packed = high + pltpu.roll(mid, PART, 1) + pltpu.roll(low, 2 * PART, 1)
    return packed.astype(BF16)


def gather_spread(packed):
    wide = packed.astype(F32)
    low = pltpu.roll(wide, LANES - 2 * PART, 1)
    mid = pltpu.roll(wide, LANES - PART, 1)
    return wide + (mid + low)


def kernel(
    nseg,
    nrep,
    heads,
    rows_ref,
    gain_ref,
    wq_hbm,
    k_hbm,
    ks_ref,
    v_hbm,
    vs_ref,
    len_ref,
    wo_hbm,
    out_ref,
    wq,
    wo,
    kbuf,
    vbuf,
    xg,
    y,
    pq,
    pq_in,
    pq32,
    squares,
    inverse,
    qs,
    oout,
    crossed_in,
    merged,
    merged_in,
    ag,
    pf,
    pf32,
    rbuf,
    sbuf,
    fbuf,
    fin,
    land,
    local_sem,
    send_sem,
    recv_sem,
):
    seg = lax.axis_index("seg")
    rep = lax.axis_index("rep")
    nrow, c = rows_ref.shape
    width = gain_ref.shape[1]
    lane = lax.broadcasted_iota(jnp.int32, (nrow, LANES), 1)
    diagonal = lane == lax.broadcasted_iota(jnp.int32, (nrow, LANES), 0)
    m = nseg // nrep
    nb = INNER_RING
    na = nseg // nb
    a, b = seg // nb, seg % nb
    hd = wq.shape[1] * nseg // heads
    hpl = LANES // hd
    hpb = c // hd
    pairs = c // LANES
    tokens = kbuf.shape[0]
    blocks = ks_ref.shape[1]
    blen = tokens // blocks

    state = {"k": 0}
    started = []

    def send(src, dst, to_rep, to_seg, start=True):
        k = state["k"]
        state["k"] += 1
        copy = pltpu.make_async_remote_copy(
            src_ref=src,
            dst_ref=dst,
            send_sem=send_sem.at[k],
            recv_sem=recv_sem.at[k],
            device_id={"rep": to_rep, "seg": to_seg},
            device_id_type=pl.DeviceIdType.MESH,
        )
        if start:
            copy.start()
            started.append(copy)
        return copy

    loads = {}
    lk = 0

    def load(name, src, dst):
        nonlocal lk
        copy = pltpu.make_async_copy(src, dst, local_sem.at[lk])
        lk += 1
        copy.start()
        loads[name] = copy

    load("wq", wq_hbm, wq)
    load("k", k_hbm.at[0], kbuf)
    load("v", v_hbm.at[0], vbuf)
    load("wo", wo_hbm, wo)

    to_rep, to_seg = seg // m, rep * m + seg % m
    alone = to_rep == rep
    barrier = pltpu.get_barrier_semaphore()

    def greet(r, s):
        pl.semaphore_signal(
            barrier, inc=1, device_id={"rep": r, "seg": s}, device_id_type=pl.DeviceIdType.MESH
        )

    for d in range(1, nseg):
        greet(rep, lax.rem(seg + d, nseg))
    for d in range(1, nrep):
        greet(lax.rem(rep + d, nrep), seg)

    @pl.when(jnp.logical_not(alone))
    def _():
        greet(to_rep, to_seg)

    pl.semaphore_wait(barrier, jnp.where(alone, nseg + nrep - 2, nseg + nrep - 1))

    first = send(rows_ref, xg.at[to_seg], to_rep, to_seg, start=False)

    @pl.when(jnp.logical_not(alone))
    def _():
        first.start()

    @pl.when(alone)
    def _():
        xg[seg] = rows_ref[...]

    wide = rows_ref[...].astype(F32)
    column = jnp.sum(wide * wide, axis=1, keepdims=True)
    across_lanes = jnp.sum(jnp.where(diagonal, column, 0.0), axis=0, keepdims=True)
    squares[seg] = jnp.broadcast_to(across_lanes, squares.shape[1:])
    shares = [
        send(squares.at[seg], squares.at[seg], rep, lax.rem(seg + d, nseg))
        for d in range(1, nseg)
    ]

    @pl.when(jnp.logical_not(alone))
    def _():
        first.wait()

    def slot(ai, bi):
        return ai * nb + bi

    def near(d):
        return lax.rem(a + d, na)

    def from_(d):
        return lax.rem(a + na - d, na)

    def gather_start(buf):
        across = [
            send(buf.at[seg], buf.at[seg], rep, slot(a, lax.rem(b + e, nb))) for e in range(1, nb)
        ]
        along = [send(buf.at[seg], buf.at[seg], rep, slot(near(d), b)) for d in range(1, na)]
        return across, along

    def pass_on(buf, d):
        block = slot(from_(d), b)
        return [
            send(buf.at[block], buf.at[block], rep, slot(a, lax.rem(b + e, nb)))
            for e in range(1, nb)
        ]

    def gather(buf, use, meanwhile=None):
        across, along = gather_start(buf)
        if meanwhile is not None:
            meanwhile()
        use(seg, 0, 0)
        waiting = [(copy, slot(a, lax.rem(b + nb - e, nb))) for e, copy in enumerate(across, 1)]
        for d, copy in enumerate(along, 1):
            copy.wait_recv()
            passed = pass_on(buf, d)
            for e, (other, block) in enumerate(waiting, 1):
                other.wait_recv()
                use(block, d - 1, e)
            use(slot(from_(d), b), d, 0)
            waiting = [
                (other, slot(from_(d), lax.rem(b + nb - e, nb))) for e, other in enumerate(passed, 1)
            ]
        for e, (other, block) in enumerate(waiting, 1):
            other.wait_recv()
            use(block, na - 1, e)

    def norms():
        for copy in shares:
            copy.wait_recv()
        total = functools.reduce(jnp.add, [squares[i] for i in range(nseg)])
        inverse[rep] = lax.rsqrt(total / width + 1e-06)
        for d in range(1, nrep):
            told.append(send(inverse.at[rep], inverse.at[rep], lax.rem(rep + d, nrep), seg))

    told = []
    gather(xg, lambda block, d, e: None, norms)
    for copy in told:
        copy.wait_recv()

    for doc in range(nrep):
        factor = jnp.sum(jnp.where(diagonal, inverse[doc][0:1], 0.0), axis=1, keepdims=True)
        for j in range(m):
            at = pl.multiple_of((rep * m + j) * c, LANES)
            y[doc * nrow : (doc + 1) * nrow, j * c : (j + 1) * c] = (
                xg[doc * m + j].astype(F32) * factor * gain_ref[0:1, pl.ds(at, c)]
            ).astype(BF16)
    loads["wq"].wait()
    part = jnp.dot(y[...], wq[...], preferred_element_type=F32)
    for doc in range(nrep):
        piece = part[doc * nrow : (doc + 1) * nrow]
        pq32[doc] = piece
        pq[doc] = piece.astype(BF16)
    sums = []
    for d in range(1, nrep):
        other = lax.rem(rep + d, nrep)
        sums.append(send(pq.at[other], pq_in.at[d - 1], other, seg))
    acc = pq32[rep]
    for d, copy in enumerate(sums):
        copy.wait_recv()
        acc = acc + pq_in[d].astype(F32)
    qs[seg] = acc.astype(BF16)

    loads["k"].wait()
    loads["v"].wait()
    position = seg * tokens + lax.broadcasted_iota(jnp.int32, (1, tokens), 1)
    bias = jnp.where(position < len_ref[0], 0.0, -1e30).astype(F32)
    def attend(block):
        def one(t, stats):
            at = pl.multiple_of(t * LANES, LANES)
            wat = pl.multiple_of(block * c + t * LANES, LANES)
            q = qs[block, :, pl.ds(at, LANES)]
            stacked = jnp.concatenate(
                [
                    jnp.where((lane >= i * hd) & (lane < (i + 1) * hd), q, jnp.zeros_like(q))
                    for i in range(hpl)
                ],
                axis=0,
            )
            scores = lax.dot_general(
                stacked,
                kbuf[:, pl.ds(wat, LANES)],
                (((1,), (1,)), ((), ())),
                preferred_element_type=F32,
            )
            scaled_rows = []
            for i in range(hpl):
                head = block * hpb + t * hpl + i
                pieces = []
                for n in range(blocks):
                    cut = slice(n * blen, (n + 1) * blen)
                    pieces.append(
                        scores[i * nrow : (i + 1) * nrow, cut] * ks_ref[0, n, head]
                        + bias[:, cut]
                    )
                top = functools.reduce(jnp.maximum, pieces)
                peak = jnp.max(top, axis=1, keepdims=True)
                weights = [jnp.exp(piece - peak) for piece in pieces]
                whole = jnp.sum(functools.reduce(jnp.add, weights), axis=1, keepdims=True)
                scaled_rows.append(
                    jnp.concatenate(
                        [(w * vs_ref[0, n, head]).astype(BF16) for n, w in enumerate(weights)],
                        axis=1,
                    )
                )
                index = t * hpl + i
                stats = jnp.where(lane == index, peak, stats)
                stats = jnp.where(lane == LANES // 2 + index, whole, stats)
            summed = jnp.dot(
                jnp.concatenate(scaled_rows, axis=0),
                vbuf[:, pl.ds(wat, LANES)],
                preferred_element_type=F32,
            )
            mine = summed[:nrow]
            for i in range(1, hpl):
                mine = jnp.where(lane >= i * hd, summed[i * nrow : (i + 1) * nrow], mine)
            oout[block, :, pl.ds(at, LANES)] = mine.astype(BF16)
            return stats

        stats = lax.fori_loop(
            0, pairs, one, jnp.zeros((nrow, LANES), F32), unroll=2 if pairs % 2 == 0 else 1
        )
        oout[block, :, c:] = spread(stats)

    def merge(parts):
        stats = [gather_spread(part_ref[:, c:]) for part_ref in parts]
        largest = functools.reduce(jnp.maximum, stats)
        factors = [jnp.exp(s - largest) for s in stats]
        totals = functools.reduce(
            jnp.add, [f * pltpu.roll(s, LANES // 2, 1) for f, s in zip(factors, stats)]
        )
        return factors, largest, totals

    def mix(factors, parts, t):
        cut = slice(t * LANES, (t + 1) * LANES)
        total = None
        for f, part_ref in zip(factors, parts):
            g = f[:, t * hpl : t * hpl + 1]
            for i in range(1, hpl):
                g = jnp.where(lane >= i * hd, f[:, t * hpl + i : t * hpl + i + 1], g)
            term = g * part_ref[:, cut].astype(F32)
            total = term if total is None else total + term
        return total

    crossing, moving = {}, []

    def settle(d):
        for copy in crossing[d]:
            copy.wait_recv()
        block = slot(from_(d), b)
        parts = [oout.at[block]] + [crossed_in.at[d, e] for e in range(nb - 1)]
        factors, largest, totals = merge(parts)
        for t in range(pairs):
            merged[d, :, t * LANES : (t + 1) * LANES] = mix(factors, parts, t).astype(BF16)
        kept = jnp.where(lane < hpb, largest, 0.0)
        kept = kept + pltpu.roll(jnp.where(lane < hpb, totals, 0.0), LANES // 2, 1)
        merged[d, :, c:] = spread(kept)
        if d:
            moving.append(send(merged.at[d], merged_in.at[d - 1], rep, block))

    def turn(block, d, e):
        attend(block)
        if e:
            to = slot(a, lax.rem(b + nb - e, nb))
            crossing.setdefault(d, []).append(
                send(oout.at[block], crossed_in.at[d, e - 1], rep, to)
            )
            if e == nb - 1 and d >= 2:
                settle(d - 1)

    gather(qs, turn)
    for d in [na - 1] * (na > 1) + [0]:
        settle(d)

    for copy in moving:
        copy.wait_recv()
    parts = [merged.at[0]] + [merged_in.at[i] for i in range(na - 1)]
    factors, _, totals = merge(parts)
    factors = [f / totals for f in factors]
    for t in range(pairs):
        ag[rep, :, t * LANES : (t + 1) * LANES] = mix(factors, parts, t).astype(BF16)
    shared = [
        send(ag.at[rep], ag.at[rep], lax.rem(rep + d, nrep), seg) for d in range(1, nrep)
    ]
    loads["wo"].wait()
    for copy in shared:
        copy.wait_recv()

    part = jnp.dot(
        ag[...].reshape(nrep * nrow, c), wo[...], preferred_element_type=F32
    )
    for p in range(nseg):
        doc, j = p // m, p % m
        piece = part[doc * nrow : (doc + 1) * nrow, j * c : (j + 1) * c]
        pf32[p] = piece
        pf[p] = piece.astype(BF16)
    order = list(range(1, na)) + [0]
    crossed = {}
    for d in order:
        crossed[d] = [
            send(
                pf.at[slot(near(d), lax.rem(b + e, nb))],
                rbuf.at[d, e - 1],
                rep,
                slot(a, lax.rem(b + e, nb)),
            )
            for e in range(1, nb)
        ]
    along = []
    for d in order:
        total = pf32[slot(near(d), b)]
        for e, copy in enumerate(crossed[d]):
            copy.wait_recv()
            total = total + rbuf[d, e].astype(F32)
        if d:
            sbuf[d - 1] = total.astype(BF16)
            along.append(send(sbuf.at[d - 1], fbuf.at[d - 1], rep, slot(near(d), b)))
    for d, copy in enumerate(along):
        copy.wait_recv()
        total = total + fbuf[d].astype(F32)
    fin[...] = total.astype(BF16)
    last = send(fin, land, to_rep, to_seg, start=False)

    @pl.when(jnp.logical_not(alone))
    def _():
        last.start()
        last.wait()
        out_ref[...] = land[...]

    @pl.when(alone)
    def _():
        out_ref[...] = fin[...]

    for copy in started:
        copy.wait_send()


def per_device(
    decoder_rows,
    norm_gain,
    query_weight,
    key_codes,
    key_scale,
    value_codes,
    value_scale,
    enc_lengths,
    output_weight,
):
    nseg, nrep = lax.axis_size("seg"), lax.axis_size("rep")
    nrow, c = decoder_rows.shape
    heads = key_scale.shape[2]
    tokens, inner = key_codes.shape[1:]
    assert key_codes.shape[0] == 1 and nseg % nrep == 0 and nseg % INNER_RING == 0
    na, nb = nseg // INNER_RING, INNER_RING
    copies = 2 + 5 * (nseg - 1) + 3 * (nrep - 1)
    vmem, smem, hbm = (
        pl.BlockSpec(memory_space=pltpu.VMEM),
        pl.BlockSpec(memory_space=pltpu.SMEM),
        pl.BlockSpec(memory_space=pl.ANY),
    )
    return pl.pallas_call(
        functools.partial(kernel, nseg, nrep, heads),
        out_shape=jax.ShapeDtypeStruct((nrow, c), BF16),
        in_specs=[vmem, vmem, hbm, hbm, smem, hbm, smem, smem, hbm],
        out_specs=vmem,
        scratch_shapes=[
            pltpu.VMEM(query_weight.shape, BF16),
            pltpu.VMEM(output_weight.shape, BF16),
            pltpu.VMEM((tokens, inner), BF16),
            pltpu.VMEM((tokens, inner), BF16),
            pltpu.VMEM((nseg, nrow, c), BF16),
            pltpu.VMEM((nrep * nrow, query_weight.shape[0]), BF16),
            pltpu.VMEM((nrep, nrow, c), BF16),
            pltpu.VMEM((nrep - 1, nrow, c), BF16),
            pltpu.VMEM((nrep, nrow, c), F32),
            pltpu.VMEM((nseg, 8, LANES), F32),
            pltpu.VMEM((nrep, 8, LANES), F32),
            pltpu.VMEM((nseg, nrow, c), BF16),
            pltpu.VMEM((nseg, nrow, c + LANES), BF16),
            pltpu.VMEM((na, nb - 1, nrow, c + LANES), BF16),
            pltpu.VMEM((na, nrow, c + LANES), BF16),
            pltpu.VMEM((na - 1, nrow, c + LANES), BF16),
            pltpu.VMEM((nrep, nrow, c), BF16),
            pltpu.VMEM((nseg, nrow, c), BF16),
            pltpu.VMEM((nseg, nrow, c), F32),
            pltpu.VMEM((na, nb - 1, nrow, c), BF16),
            pltpu.VMEM((na - 1, nrow, c), BF16),
            pltpu.VMEM((na - 1, nrow, c), BF16),
            pltpu.VMEM((nrow, c), BF16),
            pltpu.VMEM((nrow, c), BF16),
            pltpu.SemaphoreType.DMA((4,)),
            pltpu.SemaphoreType.DMA((copies,)),
            pltpu.SemaphoreType.DMA((copies,)),
        ],
        compiler_params=pltpu.CompilerParams(
            collective_id=0, has_side_effects=True, vmem_limit_bytes=60 * 1024 * 1024
        ),
    )(
        decoder_rows,
        norm_gain.reshape(1, -1),
        query_weight,
        key_codes,
        key_scale,
        value_codes,
        value_scale,
        enc_lengths,
        output_weight,
    )


def solution(mesh):
    placed = (
        P("rep", "seg"),
        P(),
        P("rep", "seg"),
        P("rep", "seg", None),
        P("rep", "seg", None),
        P("rep", "seg", None),
        P("rep", "seg", None),
        P("rep"),
        P("seg", "rep"),
    )
    return jax.shard_map(
        per_device, mesh=mesh, in_specs=placed, out_specs=P("rep", "seg"), check_vma=False
    )
```

```python
import functools

import jax
import jax.numpy as jnp
from jax import lax
from jax.experimental import pallas as pl
from jax.experimental.pallas import tpu as pltpu
from jax.sharding import PartitionSpec as P

F32 = jnp.float32
BF16 = jnp.bfloat16
LANES = 128
PART = 16
INNER_RING = 2
HALVES = 2


def spread(value):
    high = value.astype(BF16).astype(F32)
    rest = value - high
    mid = rest.astype(BF16).astype(F32)
    low = (rest - mid).astype(BF16).astype(F32)
    packed = high + pltpu.roll(mid, PART, 1) + pltpu.roll(low, 2 * PART, 1)
    return packed.astype(BF16)


def gather_spread(packed):
    wide = packed.astype(F32)
    low = pltpu.roll(wide, LANES - 2 * PART, 1)
    mid = pltpu.roll(wide, LANES - PART, 1)
    return wide + (mid + low)


def kernel(
    nseg,
    nrep,
    heads,
    rows_ref,
    gain_ref,
    wq_hbm,
    k_hbm,
    ks_ref,
    v_hbm,
    vs_ref,
    len_ref,
    wo_hbm,
    out_ref,
    wq,
    wo,
    kbuf,
    vbuf,
    xg,
    y,
    pq,
    pq_in,
    pq32,
    squares,
    inverse,
    qs,
    oout,
    crossed_in,
    merged,
    merged_in,
    ag,
    pf,
    pf32,
    rbuf,
    sbuf,
    fbuf,
    fin,
    land,
    local_sem,
    send_sem,
    recv_sem,
):
    seg = lax.axis_index("seg")
    rep = lax.axis_index("rep")
    all_rows, c = rows_ref.shape
    nrow = all_rows // HALVES
    width = gain_ref.shape[1]
    lane = lax.broadcasted_iota(jnp.int32, (nrow, LANES), 1)

    def diagonal(count, first_row):
        shape = (count, LANES)
        return lax.broadcasted_iota(jnp.int32, shape, 1) == first_row + lax.broadcasted_iota(
            jnp.int32, shape, 0
        )

    m = nseg // nrep
    nb = INNER_RING
    na = nseg // nb
    a, b = seg // nb, seg % nb
    hd = wq.shape[1] * nseg // heads
    hpl = LANES // hd
    hpb = c // hd
    pairs = c // LANES
    tokens = kbuf.shape[0]
    blocks = ks_ref.shape[1]
    blen = tokens // blocks

    state = {"k": 0}
    started = []

    def send(src, dst, to_rep, to_seg, start=True):
        k = state["k"]
        state["k"] += 1
        copy = pltpu.make_async_remote_copy(
            src_ref=src,
            dst_ref=dst,
            send_sem=send_sem.at[k],
            recv_sem=recv_sem.at[k],
            device_id={"rep": to_rep, "seg": to_seg},
            device_id_type=pl.DeviceIdType.MESH,
        )
        if start:
            copy.start()
            started.append(copy)
        return copy

    loads = {}
    lk = 0

    def load(name, src, dst):
        nonlocal lk
        copy = pltpu.make_async_copy(src, dst, local_sem.at[lk])
        lk += 1
        copy.start()
        loads[name] = copy

    load("wq", wq_hbm, wq)
    load("k", k_hbm.at[0], kbuf)
    load("v", v_hbm.at[0], vbuf)
    load("wo", wo_hbm, wo)

    to_rep, to_seg = seg // m, rep * m + seg % m
    alone = to_rep == rep
    barrier = pltpu.get_barrier_semaphore()

    def greet(r, s):
        pl.semaphore_signal(
            barrier, inc=1, device_id={"rep": r, "seg": s}, device_id_type=pl.DeviceIdType.MESH
        )

    for d in range(1, nseg):
        greet(rep, lax.rem(seg + d, nseg))
    for d in range(1, nrep):
        greet(lax.rem(rep + d, nrep), seg)

    @pl.when(jnp.logical_not(alone))
    def _():
        greet(to_rep, to_seg)

    pl.semaphore_wait(barrier, jnp.where(alone, nseg + nrep - 2, nseg + nrep - 1))

    firsts = [
        send(rows_ref.at[pl.ds(h * nrow, nrow)], xg.at[h, to_seg], to_rep, to_seg, start=False)
        for h in range(HALVES)
    ]

    @pl.when(jnp.logical_not(alone))
    def _():
        for first in firsts:
            first.start()

    @pl.when(alone)
    def _():
        for h in range(HALVES):
            xg[h, seg] = rows_ref[h * nrow : (h + 1) * nrow]

    wide = rows_ref[...].astype(F32)
    column = jnp.sum(wide * wide, axis=1, keepdims=True)
    across_lanes = jnp.sum(jnp.where(diagonal(all_rows, 0), column, 0.0), axis=0, keepdims=True)
    squares[seg] = jnp.broadcast_to(across_lanes, squares.shape[1:])
    shares = [
        send(squares.at[seg], squares.at[seg], rep, lax.rem(seg + d, nseg))
        for d in range(1, nseg)
    ]

    def slot(ai, bi):
        return ai * nb + bi

    def near(d):
        return lax.rem(a + d, na)

    def from_(d):
        return lax.rem(a + na - d, na)

    def gather_start(buf):
        across = [
            send(buf.at[seg], buf.at[seg], rep, slot(a, lax.rem(b + e, nb))) for e in range(1, nb)
        ]
        along = [send(buf.at[seg], buf.at[seg], rep, slot(near(d), b)) for d in range(1, na)]
        return across, along

    def pass_on(buf, d):
        block = slot(from_(d), b)
        return [
            send(buf.at[block], buf.at[block], rep, slot(a, lax.rem(b + e, nb)))
            for e in range(1, nb)
        ]

    def gather(buf, use, meanwhile=None):
        across, along = gather_start(buf)
        yield
        if meanwhile is not None:
            meanwhile()
        use(seg, 0, 0)
        waiting = [(copy, slot(a, lax.rem(b + nb - e, nb))) for e, copy in enumerate(across, 1)]
        for d, copy in enumerate(along, 1):
            copy.wait_recv()
            passed = pass_on(buf, d)
            for e, (other, block) in enumerate(waiting, 1):
                other.wait_recv()
                use(block, d - 1, e)
            yield
            use(slot(from_(d), b), d, 0)
            yield
            waiting = [
                (other, slot(from_(d), lax.rem(b + nb - e, nb))) for e, other in enumerate(passed, 1)
            ]
        for e, (other, block) in enumerate(waiting, 1):
            other.wait_recv()
            use(block, na - 1, e)

    def norms():
        for copy in shares:
            copy.wait_recv()
        total = functools.reduce(jnp.add, [squares[i] for i in range(nseg)])
        inverse[rep] = lax.rsqrt(total / width + 1e-06)
        for d in range(1, nrep):
            told.append(send(inverse.at[rep], inverse.at[rep], lax.rem(rep + d, nrep), seg))

    told = []
    known = []

    position = seg * tokens + lax.broadcasted_iota(jnp.int32, (1, tokens), 1)
    bias = jnp.where(position < len_ref[0], 0.0, -1e30).astype(F32)

    def once(name):
        if name in loads:
            loads.pop(name).wait()

    def chain(h, xg, y, pq, pq_in, pq32, qs, oout, crossed_in, merged, merged_in, ag, pf, pf32, rbuf, sbuf, fbuf, fin, land):
        @pl.when(jnp.logical_not(alone))
        def _():
            firsts[h].wait()

        yield from gather(xg, lambda block, d, e: None, norms if h == 0 else None)
        if not known:
            known.append(None)
            for copy in told:
                copy.wait_recv()

        for doc in range(nrep):
            factor = jnp.sum(jnp.where(diagonal(nrow, h * nrow), inverse[doc][0:1], 0.0), axis=1, keepdims=True)
            for j in range(m):
                at = pl.multiple_of((rep * m + j) * c, LANES)
                y[doc * nrow : (doc + 1) * nrow, j * c : (j + 1) * c] = (
                    xg[doc * m + j].astype(F32) * factor * gain_ref[0:1, pl.ds(at, c)]
                ).astype(BF16)
        once("wq")
        part = jnp.dot(y[...], wq[...], preferred_element_type=F32)
        for doc in range(nrep):
            piece = part[doc * nrow : (doc + 1) * nrow]
            pq32[doc] = piece
            pq[doc] = piece.astype(BF16)
        sums = []
        for d in range(1, nrep):
            other = lax.rem(rep + d, nrep)
            sums.append(send(pq.at[other], pq_in.at[d - 1], other, seg))
        yield
        acc = pq32[rep]
        for d, copy in enumerate(sums):
            copy.wait_recv()
            acc = acc + pq_in[d].astype(F32)
        qs[seg] = acc.astype(BF16)

        once("k")
        once("v")
        def attend(block):
            def one(t, stats):
                at = pl.multiple_of(t * LANES, LANES)
                wat = pl.multiple_of(block * c + t * LANES, LANES)
                q = qs[block, :, pl.ds(at, LANES)]
                stacked = jnp.concatenate(
                    [
                        jnp.where((lane >= i * hd) & (lane < (i + 1) * hd), q, jnp.zeros_like(q))
                        for i in range(hpl)
                    ],
                    axis=0,
                )
                scores = lax.dot_general(
                    stacked,
                    kbuf[:, pl.ds(wat, LANES)],
                    (((1,), (1,)), ((), ())),
                    preferred_element_type=F32,
                )
                scaled_rows = []
                for i in range(hpl):
                    head = block * hpb + t * hpl + i
                    pieces = []
                    for n in range(blocks):
                        cut = slice(n * blen, (n + 1) * blen)
                        pieces.append(
                            scores[i * nrow : (i + 1) * nrow, cut] * ks_ref[0, n, head]
                            + bias[:, cut]
                        )
                    top = functools.reduce(jnp.maximum, pieces)
                    peak = jnp.max(top, axis=1, keepdims=True)
                    weights = [jnp.exp(piece - peak) for piece in pieces]
                    whole = jnp.sum(functools.reduce(jnp.add, weights), axis=1, keepdims=True)
                    scaled_rows.append(
                        jnp.concatenate(
                            [(w * vs_ref[0, n, head]).astype(BF16) for n, w in enumerate(weights)],
                            axis=1,
                        )
                    )
                    index = t * hpl + i
                    stats = jnp.where(lane == index, peak, stats)
                    stats = jnp.where(lane == LANES // 2 + index, whole, stats)
                summed = jnp.dot(
                    jnp.concatenate(scaled_rows, axis=0),
                    vbuf[:, pl.ds(wat, LANES)],
                    preferred_element_type=F32,
                )
                mine = summed[:nrow]
                for i in range(1, hpl):
                    mine = jnp.where(lane >= i * hd, summed[i * nrow : (i + 1) * nrow], mine)
                oout[block, :, pl.ds(at, LANES)] = mine.astype(BF16)
                return stats

            stats = lax.fori_loop(
                0, pairs, one, jnp.zeros((nrow, LANES), F32), unroll=2 if pairs % 2 == 0 else 1
            )
            oout[block, :, c:] = spread(stats)

        def merge(parts):
            stats = [gather_spread(part_ref[:, c:]) for part_ref in parts]
            largest = functools.reduce(jnp.maximum, stats)
            factors = [jnp.exp(s - largest) for s in stats]
            totals = functools.reduce(
                jnp.add, [f * pltpu.roll(s, LANES // 2, 1) for f, s in zip(factors, stats)]
            )
            return factors, largest, totals

        def mix(factors, parts, t):
            cut = slice(t * LANES, (t + 1) * LANES)
            total = None
            for f, part_ref in zip(factors, parts):
                g = f[:, t * hpl : t * hpl + 1]
                for i in range(1, hpl):
                    g = jnp.where(lane >= i * hd, f[:, t * hpl + i : t * hpl + i + 1], g)
                term = g * part_ref[:, cut].astype(F32)
                total = term if total is None else total + term
            return total

        crossing, moving = {}, []

        def settle(d):
            for copy in crossing[d]:
                copy.wait_recv()
            block = slot(from_(d), b)
            parts = [oout.at[block]] + [crossed_in.at[d, e] for e in range(nb - 1)]
            factors, largest, totals = merge(parts)
            for t in range(pairs):
                merged[d, :, t * LANES : (t + 1) * LANES] = mix(factors, parts, t).astype(BF16)
            kept = jnp.where(lane < hpb, largest, 0.0)
            kept = kept + pltpu.roll(jnp.where(lane < hpb, totals, 0.0), LANES // 2, 1)
            merged[d, :, c:] = spread(kept)
            if d:
                moving.append(send(merged.at[d], merged_in.at[d - 1], rep, block))

        def turn(block, d, e):
            attend(block)
            if e:
                to = slot(a, lax.rem(b + nb - e, nb))
                crossing.setdefault(d, []).append(
                    send(oout.at[block], crossed_in.at[d, e - 1], rep, to)
                )
                if e == nb - 1 and d >= 2:
                    settle(d - 1)

        yield from gather(qs, turn)
        for d in [na - 1] * (na > 1) + [0]:
            yield
            settle(d)
        yield

        for copy in moving:
            copy.wait_recv()
        parts = [merged.at[0]] + [merged_in.at[i] for i in range(na - 1)]
        factors, _, totals = merge(parts)
        factors = [f / totals for f in factors]
        for t in range(pairs):
            ag[rep, :, t * LANES : (t + 1) * LANES] = mix(factors, parts, t).astype(BF16)
        shared = [
            send(ag.at[rep], ag.at[rep], lax.rem(rep + d, nrep), seg) for d in range(1, nrep)
        ]
        once("wo")
        yield
        for copy in shared:
            copy.wait_recv()

        part = jnp.dot(
            ag[...].reshape(nrep * nrow, c), wo[...], preferred_element_type=F32
        )
        for p in range(nseg):
            doc, j = p // m, p % m
            piece = part[doc * nrow : (doc + 1) * nrow, j * c : (j + 1) * c]
            pf32[p] = piece
            pf[p] = piece.astype(BF16)
        order = list(range(1, na)) + [0]
        crossed = {}
        for d in order:
            crossed[d] = [
                send(
                    pf.at[slot(near(d), lax.rem(b + e, nb))],
                    rbuf.at[d, e - 1],
                    rep,
                    slot(a, lax.rem(b + e, nb)),
                )
                for e in range(1, nb)
            ]
        along = []
        for d in order:
            yield
            total = pf32[slot(near(d), b)]
            for e, copy in enumerate(crossed[d]):
                copy.wait_recv()
                total = total + rbuf[d, e].astype(F32)
            if d:
                sbuf[d - 1] = total.astype(BF16)
                along.append(send(sbuf.at[d - 1], fbuf.at[d - 1], rep, slot(near(d), b)))
        yield
        for d, copy in enumerate(along):
            copy.wait_recv()
            total = total + fbuf[d].astype(F32)
        fin[...] = total.astype(BF16)
        last = send(fin, land, to_rep, to_seg, start=False)
        mine = pl.ds(h * nrow, nrow)

        @pl.when(jnp.logical_not(alone))
        def _():
            last.start()

        yield

        @pl.when(jnp.logical_not(alone))
        def _():
            last.wait()
            out_ref[mine, :] = land[...]

        @pl.when(alone)
        def _():
            out_ref[mine, :] = fin[...]


    state_refs = [xg, y, pq, pq_in, pq32, qs, oout, crossed_in, merged, merged_in, ag, pf, pf32, rbuf, sbuf, fbuf, fin, land]
    chains = [chain(h, *[ref.at[h] for ref in state_refs]) for h in range(HALVES)]
    while chains:
        for steps in list(chains):
            try:
                next(steps)
            except StopIteration:
                chains.remove(steps)
    for name in list(loads):
        once(name)
    for copy in started:
        copy.wait_send()


def per_device(
    decoder_rows,
    norm_gain,
    query_weight,
    key_codes,
    key_scale,
    value_codes,
    value_scale,
    enc_lengths,
    output_weight,
):
    nseg, nrep = lax.axis_size("seg"), lax.axis_size("rep")
    nrow, c = decoder_rows.shape
    heads = key_scale.shape[2]
    tokens, inner = key_codes.shape[1:]
    assert key_codes.shape[0] == 1 and nseg % nrep == 0 and nseg % INNER_RING == 0
    na, nb = nseg // INNER_RING, INNER_RING
    copies = HALVES * (2 + 4 * (nseg - 1) + 2 * (nrep - 1)) + nseg - 1 + nrep - 1
    part = nrow // HALVES

    def half(shape, dtype=BF16):
        return pltpu.VMEM((HALVES,) + shape, dtype)

    vmem, smem, hbm = (
        pl.BlockSpec(memory_space=pltpu.VMEM),
        pl.BlockSpec(memory_space=pltpu.SMEM),
        pl.BlockSpec(memory_space=pl.ANY),
    )
    return pl.pallas_call(
        functools.partial(kernel, nseg, nrep, heads),
        out_shape=jax.ShapeDtypeStruct((nrow, c), BF16),
        in_specs=[vmem, vmem, hbm, hbm, smem, hbm, smem, smem, hbm],
        out_specs=vmem,
        scratch_shapes=[
            pltpu.VMEM(query_weight.shape, BF16),
            pltpu.VMEM(output_weight.shape, BF16),
            pltpu.VMEM((tokens, inner), BF16),
            pltpu.VMEM((tokens, inner), BF16),
            half((nseg, part, c)),
            half((nrep * part, query_weight.shape[0])),
            half((nrep, part, c)),
            half((nrep - 1, part, c)),
            half((nrep, part, c), F32),
            pltpu.VMEM((nseg, 8, LANES), F32),
            pltpu.VMEM((nrep, 8, LANES), F32),
            half((nseg, part, c)),
            half((nseg, part, c + LANES)),
            half((na, nb - 1, part, c + LANES)),
            half((na, part, c + LANES)),
            half((na - 1, part, c + LANES)),
            half((nrep, part, c)),
            half((nseg, part, c)),
            half((nseg, part, c), F32),
            half((na, nb - 1, part, c)),
            half((na - 1, part, c)),
            half((na - 1, part, c)),
            half((part, c)),
            half((part, c)),
            pltpu.SemaphoreType.DMA((4,)),
            pltpu.SemaphoreType.DMA((copies,)),
            pltpu.SemaphoreType.DMA((copies,)),
        ],
        compiler_params=pltpu.CompilerParams(
            collective_id=0, has_side_effects=True, vmem_limit_bytes=60 * 1024 * 1024
        ),
    )(
        decoder_rows,
        norm_gain.reshape(1, -1),
        query_weight,
        key_codes,
        key_scale,
        value_codes,
        value_scale,
        enc_lengths,
        output_weight,
    )


def solution(mesh):
    placed = (
        P("rep", "seg"),
        P(),
        P("rep", "seg"),
        P("rep", "seg", None),
        P("rep", "seg", None),
        P("rep", "seg", None),
        P("rep", "seg", None),
        P("rep"),
        P("seg", "rep"),
    )
    return jax.shard_map(
        per_device, mesh=mesh, in_specs=placed, out_specs=P("rep", "seg"), check_vma=False
    )
```

```python
import functools

import jax
import jax.numpy as jnp
from jax import lax
from jax.experimental import pallas as pl
from jax.experimental.pallas import tpu as pltpu
from jax.sharding import PartitionSpec as P

F32 = jnp.float32
BF16 = jnp.bfloat16
LANES = 128
PART = 16
INNER_RING = 2


def spread(value):
    high = value.astype(BF16).astype(F32)
    rest = value - high
    mid = rest.astype(BF16).astype(F32)
    low = (rest - mid).astype(BF16).astype(F32)
    packed = high + pltpu.roll(mid, PART, 1) + pltpu.roll(low, 2 * PART, 1)
    return packed.astype(BF16)


def gather_spread(packed):
    wide = packed.astype(F32)
    low = pltpu.roll(wide, LANES - 2 * PART, 1)
    mid = pltpu.roll(wide, LANES - PART, 1)
    return wide + (mid + low)


def kernel(
    nseg,
    nrep,
    heads,
    rows_ref,
    gain_ref,
    wq_hbm,
    k_hbm,
    ks_ref,
    v_hbm,
    vs_ref,
    len_ref,
    wo_hbm,
    out_ref,
    wq,
    wo,
    kbuf,
    vbuf,
    xg,
    y,
    pq,
    pq_in,
    pq32,
    squares,
    inverse,
    qs,
    oout,
    crossed_in,
    merged,
    merged_in,
    ag,
    pf,
    pf32,
    rbuf,
    sbuf,
    fbuf,
    fin,
    land,
    local_sem,
    send_sem,
    recv_sem,
):
    seg = lax.axis_index("seg")
    rep = lax.axis_index("rep")
    nrow, c = rows_ref.shape
    width = gain_ref.shape[1]
    lane = lax.broadcasted_iota(jnp.int32, (nrow, LANES), 1)
    diagonal = lane == lax.broadcasted_iota(jnp.int32, (nrow, LANES), 0)
    m = nseg // nrep
    nb = INNER_RING
    na = nseg // nb
    a, b = seg // nb, seg % nb
    hd = wq.shape[1] * nseg // heads
    hpl = LANES // hd
    hpb = c // hd
    pairs = c // LANES
    tokens = kbuf.shape[0]
    blocks = ks_ref.shape[1]
    blen = tokens // blocks

    state = {"k": 0}
    started = []

    def send(src, dst, to_rep, to_seg, start=True):
        k = state["k"]
        state["k"] += 1
        copy = pltpu.make_async_remote_copy(
            src_ref=src,
            dst_ref=dst,
            send_sem=send_sem.at[k],
            recv_sem=recv_sem.at[k],
            device_id={"rep": to_rep, "seg": to_seg},
            device_id_type=pl.DeviceIdType.MESH,
        )
        if start:
            copy.start()
            started.append(copy)
        return copy

    loads = {}
    lk = 0

    def load(name, src, dst):
        nonlocal lk
        copy = pltpu.make_async_copy(src, dst, local_sem.at[lk])
        lk += 1
        copy.start()
        loads[name] = copy

    load("wq", wq_hbm, wq)
    load("k", k_hbm.at[0], kbuf)
    load("v", v_hbm.at[0], vbuf)
    load("wo", wo_hbm, wo)

    to_rep, to_seg = seg // m, rep * m + seg % m
    alone = to_rep == rep
    barrier = pltpu.get_barrier_semaphore()

    def greet(r, s):
        pl.semaphore_signal(
            barrier, inc=1, device_id={"rep": r, "seg": s}, device_id_type=pl.DeviceIdType.MESH
        )

    for d in range(1, nseg):
        greet(rep, lax.rem(seg + d, nseg))
    for d in range(1, nrep):
        greet(lax.rem(rep + d, nrep), seg)

    @pl.when(jnp.logical_not(alone))
    def _():
        greet(to_rep, to_seg)

    pl.semaphore_wait(barrier, jnp.where(alone, nseg + nrep - 2, nseg + nrep - 1))

    first = send(rows_ref, xg.at[to_seg], to_rep, to_seg, start=False)

    @pl.when(jnp.logical_not(alone))
    def _():
        first.start()

    @pl.when(alone)
    def _():
        xg[seg] = rows_ref[...]

    wide = rows_ref[...].astype(F32)
    column = jnp.sum(wide * wide, axis=1, keepdims=True)
    across_lanes = jnp.sum(jnp.where(diagonal, column, 0.0), axis=0, keepdims=True)
    squares[seg] = jnp.broadcast_to(across_lanes, squares.shape[1:])
    shares = [
        send(squares.at[seg], squares.at[seg], rep, lax.rem(seg + d, nseg))
        for d in range(1, nseg)
    ]

    @pl.when(jnp.logical_not(alone))
    def _():
        first.wait()

    def slot(ai, bi):
        return ai * nb + bi

    def near(d):
        if na & (na - 1):
            return lax.rem(a + d, na)
        flipped, bit = 0, 1
        while bit < na:
            own = (a // bit) % 2
            flipped = flipped + bit * ((1 - own) if d & bit else own)
            bit *= 2
        return flipped

    def from_(d):
        return lax.rem(a + na - d, na) if na & (na - 1) else near(d)

    def gather_start(buf):
        across = [
            send(buf.at[seg], buf.at[seg], rep, slot(a, lax.rem(b + e, nb))) for e in range(1, nb)
        ]
        along = [send(buf.at[seg], buf.at[seg], rep, slot(near(d), b)) for d in range(1, na)]
        return across, along

    def pass_on(buf, d):
        block = slot(from_(d), b)
        return [
            send(buf.at[block], buf.at[block], rep, slot(a, lax.rem(b + e, nb)))
            for e in range(1, nb)
        ]

    def gather(buf, use, meanwhile=None):
        across, along = gather_start(buf)
        if meanwhile is not None:
            meanwhile()
        use(seg, 0, 0)
        waiting = [(copy, slot(a, lax.rem(b + nb - e, nb))) for e, copy in enumerate(across, 1)]
        for d, copy in enumerate(along, 1):
            copy.wait_recv()
            passed = pass_on(buf, d)
            for e, (other, block) in enumerate(waiting, 1):
                other.wait_recv()
                use(block, d - 1, e)
            use(slot(from_(d), b), d, 0)
            waiting = [
                (other, slot(from_(d), lax.rem(b + nb - e, nb))) for e, other in enumerate(passed, 1)
            ]
        for e, (other, block) in enumerate(waiting, 1):
            other.wait_recv()
            use(block, na - 1, e)

    def norms():
        for copy in shares:
            copy.wait_recv()
        total = functools.reduce(jnp.add, [squares[i] for i in range(nseg)])
        inverse[rep] = lax.rsqrt(total / width + 1e-06)
        for d in range(1, nrep):
            told.append(send(inverse.at[rep], inverse.at[rep], lax.rem(rep + d, nrep), seg))

    told = []
    gather(xg, lambda block, d, e: None, norms)
    for copy in told:
        copy.wait_recv()

    for doc in range(nrep):
        factor = jnp.sum(jnp.where(diagonal, inverse[doc][0:1], 0.0), axis=1, keepdims=True)
        for j in range(m):
            at = pl.multiple_of((rep * m + j) * c, LANES)
            y[doc * nrow : (doc + 1) * nrow, j * c : (j + 1) * c] = (
                xg[doc * m + j].astype(F32) * factor * gain_ref[0:1, pl.ds(at, c)]
            ).astype(BF16)
    loads["wq"].wait()
    part = jnp.dot(y[...], wq[...], preferred_element_type=F32)
    for doc in range(nrep):
        piece = part[doc * nrow : (doc + 1) * nrow]
        pq32[doc] = piece
        pq[doc] = piece.astype(BF16)
    sums = []
    for d in range(1, nrep):
        other = lax.rem(rep + d, nrep)
        sums.append(send(pq.at[other], pq_in.at[d - 1], other, seg))
    acc = pq32[rep]
    for d, copy in enumerate(sums):
        copy.wait_recv()
        acc = acc + pq_in[d].astype(F32)
    qs[seg] = acc.astype(BF16)

    loads["k"].wait()
    loads["v"].wait()
    position = seg * tokens + lax.broadcasted_iota(jnp.int32, (1, tokens), 1)
    bias = jnp.where(position < len_ref[0], 0.0, -1e30).astype(F32)
    def attend(block):
        def one(t, stats):
            at = pl.multiple_of(t * LANES, LANES)
            wat = pl.multiple_of(block * c + t * LANES, LANES)
            q = qs[block, :, pl.ds(at, LANES)]
            stacked = jnp.concatenate(
                [
                    jnp.where((lane >= i * hd) & (lane < (i + 1) * hd), q, jnp.zeros_like(q))
                    for i in range(hpl)
                ],
                axis=0,
            )
            scores = lax.dot_general(
                stacked,
                kbuf[:, pl.ds(wat, LANES)],
                (((1,), (1,)), ((), ())),
                preferred_element_type=F32,
            )
            scaled_rows = []
            for i in range(hpl):
                head = block * hpb + t * hpl + i
                pieces = []
                for n in range(blocks):
                    cut = slice(n * blen, (n + 1) * blen)
                    pieces.append(
                        scores[i * nrow : (i + 1) * nrow, cut] * ks_ref[0, n, head]
                        + bias[:, cut]
                    )
                top = functools.reduce(jnp.maximum, pieces)
                peak = jnp.max(top, axis=1, keepdims=True)
                weights = [jnp.exp(piece - peak) for piece in pieces]
                whole = jnp.sum(functools.reduce(jnp.add, weights), axis=1, keepdims=True)
                scaled_rows.append(
                    jnp.concatenate(
                        [(w * vs_ref[0, n, head]).astype(BF16) for n, w in enumerate(weights)],
                        axis=1,
                    )
                )
                index = t * hpl + i
                stats = jnp.where(lane == index, peak, stats)
                stats = jnp.where(lane == LANES // 2 + index, whole, stats)
            summed = jnp.dot(
                jnp.concatenate(scaled_rows, axis=0),
                vbuf[:, pl.ds(wat, LANES)],
                preferred_element_type=F32,
            )
            mine = summed[:nrow]
            for i in range(1, hpl):
                mine = jnp.where(lane >= i * hd, summed[i * nrow : (i + 1) * nrow], mine)
            oout[block, :, pl.ds(at, LANES)] = mine.astype(BF16)
            return stats

        stats = lax.fori_loop(
            0, pairs, one, jnp.zeros((nrow, LANES), F32), unroll=2 if pairs % 2 == 0 else 1
        )
        oout[block, :, c:] = spread(stats)

    def merge(parts):
        stats = [gather_spread(part_ref[:, c:]) for part_ref in parts]
        largest = functools.reduce(jnp.maximum, stats)
        factors = [jnp.exp(s - largest) for s in stats]
        totals = functools.reduce(
            jnp.add, [f * pltpu.roll(s, LANES // 2, 1) for f, s in zip(factors, stats)]
        )
        return factors, largest, totals

    def mix(factors, parts, t):
        cut = slice(t * LANES, (t + 1) * LANES)
        total = None
        for f, part_ref in zip(factors, parts):
            g = f[:, t * hpl : t * hpl + 1]
            for i in range(1, hpl):
                g = jnp.where(lane >= i * hd, f[:, t * hpl + i : t * hpl + i + 1], g)
            term = g * part_ref[:, cut].astype(F32)
            total = term if total is None else total + term
        return total

    crossing, moving = {}, []

    def settle(d):
        for copy in crossing[d]:
            copy.wait_recv()
        block = slot(from_(d), b)
        parts = [oout.at[block]] + [crossed_in.at[d, e] for e in range(nb - 1)]
        factors, largest, totals = merge(parts)
        for t in range(pairs):
            merged[d, :, t * LANES : (t + 1) * LANES] = mix(factors, parts, t).astype(BF16)
        kept = jnp.where(lane < hpb, largest, 0.0)
        kept = kept + pltpu.roll(jnp.where(lane < hpb, totals, 0.0), LANES // 2, 1)
        merged[d, :, c:] = spread(kept)
        if d:
            moving.append(send(merged.at[d], merged_in.at[d - 1], rep, block))

    def turn(block, d, e):
        attend(block)
        if e:
            to = slot(a, lax.rem(b + nb - e, nb))
            crossing.setdefault(d, []).append(
                send(oout.at[block], crossed_in.at[d, e - 1], rep, to)
            )
            if e == nb - 1 and d >= 2:
                settle(d - 1)

    gather(qs, turn)
    for d in [na - 1] * (na > 1) + [0]:
        settle(d)

    for copy in moving:
        copy.wait_recv()
    parts = [merged.at[0]] + [merged_in.at[i] for i in range(na - 1)]
    factors, _, totals = merge(parts)
    factors = [f / totals for f in factors]
    for t in range(pairs):
        ag[rep, :, t * LANES : (t + 1) * LANES] = mix(factors, parts, t).astype(BF16)
    shared = [
        send(ag.at[rep], ag.at[rep], lax.rem(rep + d, nrep), seg) for d in range(1, nrep)
    ]
    loads["wo"].wait()
    for copy in shared:
        copy.wait_recv()

    part = jnp.dot(
        ag[...].reshape(nrep * nrow, c), wo[...], preferred_element_type=F32
    )
    for p in range(nseg):
        doc, j = p // m, p % m
        piece = part[doc * nrow : (doc + 1) * nrow, j * c : (j + 1) * c]
        pf32[p] = piece
        pf[p] = piece.astype(BF16)
    order = list(range(na - 1, -1, -1))
    crossed = {}
    for d in order:
        crossed[d] = [
            send(
                pf.at[slot(near(d), lax.rem(b + e, nb))],
                rbuf.at[d, e - 1],
                rep,
                slot(a, lax.rem(b + e, nb)),
            )
            for e in range(1, nb)
        ]
    along = []
    for d in order:
        total = pf32[slot(near(d), b)]
        for e, copy in enumerate(crossed[d]):
            copy.wait_recv()
            total = total + rbuf[d, e].astype(F32)
        if d:
            sbuf[d - 1] = total.astype(BF16)
            along.append(send(sbuf.at[d - 1], fbuf.at[d - 1], rep, slot(near(d), b)))
    for copy in along:
        copy.wait_recv()
    for d in range(na - 1):
        total = total + fbuf[d].astype(F32)
    fin[...] = total.astype(BF16)
    last = send(fin, land, to_rep, to_seg, start=False)

    @pl.when(jnp.logical_not(alone))
    def _():
        last.start()
        last.wait()
        out_ref[...] = land[...]

    @pl.when(alone)
    def _():
        out_ref[...] = fin[...]

    for copy in started:
        copy.wait_send()


def per_device(
    decoder_rows,
    norm_gain,
    query_weight,
    key_codes,
    key_scale,
    value_codes,
    value_scale,
    enc_lengths,
    output_weight,
):
    nseg, nrep = lax.axis_size("seg"), lax.axis_size("rep")
    nrow, c = decoder_rows.shape
    heads = key_scale.shape[2]
    tokens, inner = key_codes.shape[1:]
    assert key_codes.shape[0] == 1 and nseg % nrep == 0 and nseg % INNER_RING == 0
    na, nb = nseg // INNER_RING, INNER_RING
    copies = 2 + 5 * (nseg - 1) + 3 * (nrep - 1)
    vmem, smem, hbm = (
        pl.BlockSpec(memory_space=pltpu.VMEM),
        pl.BlockSpec(memory_space=pltpu.SMEM),
        pl.BlockSpec(memory_space=pl.ANY),
    )
    return pl.pallas_call(
        functools.partial(kernel, nseg, nrep, heads),
        out_shape=jax.ShapeDtypeStruct((nrow, c), BF16),
        in_specs=[vmem, vmem, hbm, hbm, smem, hbm, smem, smem, hbm],
        out_specs=vmem,
        scratch_shapes=[
            pltpu.VMEM(query_weight.shape, BF16),
            pltpu.VMEM(output_weight.shape, BF16),
            pltpu.VMEM((tokens, inner), BF16),
            pltpu.VMEM((tokens, inner), BF16),
            pltpu.VMEM((nseg, nrow, c), BF16),
            pltpu.VMEM((nrep * nrow, query_weight.shape[0]), BF16),
            pltpu.VMEM((nrep, nrow, c), BF16),
            pltpu.VMEM((nrep - 1, nrow, c), BF16),
            pltpu.VMEM((nrep, nrow, c), F32),
            pltpu.VMEM((nseg, 8, LANES), F32),
            pltpu.VMEM((nrep, 8, LANES), F32),
            pltpu.VMEM((nseg, nrow, c), BF16),
            pltpu.VMEM((nseg, nrow, c + LANES), BF16),
            pltpu.VMEM((na, nb - 1, nrow, c + LANES), BF16),
            pltpu.VMEM((na, nrow, c + LANES), BF16),
            pltpu.VMEM((na - 1, nrow, c + LANES), BF16),
            pltpu.VMEM((nrep, nrow, c), BF16),
            pltpu.VMEM((nseg, nrow, c), BF16),
            pltpu.VMEM((nseg, nrow, c), F32),
            pltpu.VMEM((na, nb - 1, nrow, c), BF16),
            pltpu.VMEM((na - 1, nrow, c), BF16),
            pltpu.VMEM((na - 1, nrow, c), BF16),
            pltpu.VMEM((nrow, c), BF16),
            pltpu.VMEM((nrow, c), BF16),
            pltpu.SemaphoreType.DMA((4,)),
            pltpu.SemaphoreType.DMA((copies,)),
            pltpu.SemaphoreType.DMA((copies,)),
        ],
        compiler_params=pltpu.CompilerParams(
            collective_id=0, has_side_effects=True, vmem_limit_bytes=60 * 1024 * 1024
        ),
    )(
        decoder_rows,
        norm_gain.reshape(1, -1),
        query_weight,
        key_codes,
        key_scale,
        value_codes,
        value_scale,
        enc_lengths,
        output_weight,
    )


def solution(mesh):
    placed = (
        P("rep", "seg"),
        P(),
        P("rep", "seg"),
        P("rep", "seg", None),
        P("rep", "seg", None),
        P("rep", "seg", None),
        P("rep", "seg", None),
        P("rep"),
        P("seg", "rep"),
    )
    return jax.shard_map(
        per_device, mesh=mesh, in_specs=placed, out_specs=P("rep", "seg"), check_vma=False
    )
```
